32 devices in a mesh: alpha: 8 (over z, x), beta: 4 (over y, core).
Axes of the slice: x: 2, y: 2, z: 4, core: 2. Of those that a mesh axis runs over, the one named last changes fastest.
Arguments:
- coeffs: bfloat16 [2048, 4096], P('alpha', 'beta'), may hold values from -6 to 6
- a_blocks: bfloat16 [2, 2048, 11, 128], P(None, 'alpha'), may hold values from -0.15625 to 0.15625
- a_list: int32 [2, 16, 11], replicated, may hold values from 0 to 15, as said below
- a_count: int32 [2, 16], replicated, may hold values from 4 to 11, as said below
- b_blocks: bfloat16 [2, 4096, 11, 128], P(None, 'beta'), may hold values from -0.15625 to 0.15625
- b_list: int32 [2, 32, 11], replicated, may hold values from 0 to 31, as said below
- b_count: int32 [2, 32], replicated, may hold values from 4 to 11, as said below
Outputs:
- sigma: float32 [2048, 4096], P('alpha', 'beta')
The draws below stay inside these ranges and needn't reach their ends.
Inputs may be any that keep to these rules, and one draw needn't show every extreme that they name: `a_list`: every entry, valid slot or not, is an alpha block number. For each index r of alpha and each index o of alpha, the entries of all operators in the rows of blocks r * 2 to r * 2 + 1 that lie in blocks o * 2 to o * 2 + 1 name at most 1 distinct blocks, and some pair names exactly 1. `b_list`: the same with beta, 8 and 2. `a_count`: some row has all 11 slots valid. `b_count`: some row has all 11 slots valid.
All inputs are finite; a program needn't handle non-finite values.
Results may differ from the reference program's by a relative error of at most 0.0029.
Values may be sent and summed in bfloat16 or wider, within the bound.
A program may use at most 128 MiB of HBM per device.

```python
import jax
import jax.numpy as jnp
from jax import lax

BLOCK = 128
ABLK_DEV = 2
BBLK_DEV = 8
LIST = 11
OPS = 2
NA = 2048
NB = 4096
FROM_A = 1
FROM_B = 2
N_ALPHA = 8
N_BETA = 4


def listed_blocks(key, owners, per_owner, capacity):
    score_key = jax.random.fold_in(key, 101)
    pick_key = jax.random.fold_in(key, 202)
    scores = jax.random.randint(score_key, (owners, owners, per_owner), 0, 1 << 20)
    scores = scores * per_owner + jnp.arange(per_owner, dtype=jnp.int32)
    ordering = jnp.argsort(scores, axis=-1, stable=True)[..., :capacity].astype(jnp.int32)
    allowed = ordering + (jnp.arange(owners, dtype=jnp.int32) * per_owner)[None, :, None]
    allowed = allowed.reshape(owners, owners * capacity)
    picks = jax.random.randint(pick_key, (OPS, owners, per_owner, LIST), 0, owners * capacity)
    receivers = jnp.arange(owners, dtype=jnp.int32)[None, :, None, None]
    entries = allowed[receivers, picks]
    entries = entries.at[0, 0, 0, :capacity].set(allowed[0, :capacity])
    return entries.reshape(OPS, owners * per_owner, LIST).astype(jnp.int32)


def valid_counts(key, total):
    counts = jax.random.randint(key, (OPS, total), LIST // 3 + 1, LIST + 1)
    return counts.at[0, 0].set(LIST).astype(jnp.int32)


def draw_a_list(key, part):
    return listed_blocks(jax.random.fold_in(key, 11), N_ALPHA, ABLK_DEV, FROM_A)


def draw_b_list(key, part):
    return listed_blocks(jax.random.fold_in(key, 12), N_BETA, BBLK_DEV, FROM_B)


def draw_a_count(key, part):
    return valid_counts(jax.random.fold_in(key, 21), ABLK_DEV * N_ALPHA)


def draw_b_count(key, part):
    return valid_counts(jax.random.fold_in(key, 22), BBLK_DEV * N_BETA)


def level_of(own_key, dims, cuts, low, high):
    level, own = 1.0, jax.random.fold_in(own_key, 6)
    for position, blocks in cuts:
        steps = jnp.exp(jax.random.uniform(jax.random.fold_in(own, position), (blocks,), jnp.float32, low / len(cuts), high / len(cuts)))
        level = level * jnp.repeat(steps, dims[position] // blocks).reshape([-1 if axis == position else 1 for axis in range(len(dims))])
    return level


def centred(stream_key, dims, deviation, reach, cuts=(), kind=jnp.bfloat16):
    drawn = jax.random.normal(stream_key, dims, jnp.float32) * deviation
    if len(cuts) > 0:
        drawn = level_of(stream_key, dims, cuts, -0.22, 0.18) * drawn
    return jnp.clip(drawn, min=-reach, max=reach).astype(kind)


def setup_inputs(seed: int = 0) -> dict:
    seeds = jax.random.split(jax.random.key(seed), 8)
    coeffs = centred(seeds[0], (NA, NB), 1.0, 6.0, ((0, 8), (1, 4)))
    a_blocks = centred(seeds[1], (OPS, NA, LIST, BLOCK), (LIST * BLOCK) ** -0.5, 0.15625, ((1, 8),))
    a_list = draw_a_list(jax.random.fold_in(seeds[7], 71), 0)
    a_count = draw_a_count(jax.random.fold_in(seeds[7], 71), 0)
    b_blocks = centred(seeds[4], (OPS, NB, LIST, BLOCK), (LIST * BLOCK) ** -0.5, 0.15625, ((1, 4),))
    b_list = draw_b_list(jax.random.fold_in(seeds[7], 71), 0)
    b_count = draw_b_count(jax.random.fold_in(seeds[7], 71), 0)
    return {"coeffs": coeffs, "a_blocks": a_blocks, "a_list": a_list, "a_count": a_count, "b_blocks": b_blocks, "b_list": b_list, "b_count": b_count}


def reference(coeffs, a_blocks, a_list, a_count, b_blocks, b_list, b_count):
    operators, alpha_total, list_slots, block_size = a_blocks.shape
    beta_total = coeffs.shape[1]
    alpha_nblk = alpha_total // block_size
    beta_nblk = beta_total // block_size
    slot_ids = jnp.arange(list_slots, dtype=jnp.int32)
    coeff_blocks = coeffs.reshape(alpha_nblk, block_size, beta_total)
    sigma = jnp.zeros((alpha_total, beta_total), jnp.float32)
    for k in range(operators):
        alpha_valid = slot_ids[None, :] < a_count[k][:, None]
        alpha_kept = jnp.where(alpha_valid[:, None, :, None], a_blocks[k].reshape(alpha_nblk, block_size, list_slots, block_size), jnp.zeros((), a_blocks.dtype))

        def row_block(pair):
            factor_rows, entries = pair
            picked = coeff_blocks[entries.astype(jnp.int32)].reshape(list_slots * block_size, beta_total)
            return jnp.dot(factor_rows.reshape(block_size, list_slots * block_size), picked, preferred_element_type=jnp.float32)

        inter = lax.map(row_block, (alpha_kept, a_list[k]))
        inter = inter.reshape(alpha_total, beta_total).astype(jnp.bfloat16)
        inter_cols = inter.reshape(alpha_total, beta_nblk, block_size)
        beta_valid = slot_ids[None, :] < b_count[k][:, None]
        beta_kept = jnp.where(beta_valid[:, None, :, None], b_blocks[k].reshape(beta_nblk, block_size, list_slots, block_size), jnp.zeros((), b_blocks.dtype))

        def col_block(pair):
            factor_rows, entries = pair
            picked = inter_cols[:, entries.astype(jnp.int32), :].reshape(alpha_total, list_slots * block_size)
            return jnp.dot(picked, factor_rows.reshape(block_size, list_slots * block_size).T, preferred_element_type=jnp.float32)

        partial_sigma = lax.map(col_block, (beta_kept, b_list[k]))
        sigma = sigma + jnp.transpose(partial_sigma, (1, 0, 2)).reshape(alpha_total, beta_total)
    return sigma
```

```python
import functools

import jax
import jax.numpy as jnp
from jax import lax
from jax.experimental import pallas as pl
from jax.experimental.pallas import tpu as pltpu
from jax.sharding import PartitionSpec as P

FROM_A = 1
FROM_B = 2
PAIR = 2
VMEM_LIMIT = 60 * 1024 * 1024
MESH = pl.DeviceIdType.MESH


def pick_kernel(geometry, a_lists, b_lists, c_ref, picks_ref, small):
    na, nb, ops, slots, blk, row_blocks, col_blocks = geometry
    a = lax.axis_index("alpha")
    c = lax.axis_index("beta")
    lists = b_lists[...]
    lane = lax.broadcasted_iota(jnp.int32, (1, nb * col_blocks), 1)

    def extremes(receiver, owner):
        local = lists - owner * col_blocks
        hit = (local >= 0) & (local < col_blocks)
        rows_here = (lane >= receiver * col_blocks) & (lane < (receiver + 1) * col_blocks)
        low = jnp.min(jnp.min(jnp.where(hit, local, col_blocks), axis=0), axis=0, keepdims=True)
        high = jnp.max(jnp.max(jnp.where(hit, local, 0), axis=0), axis=0, keepdims=True)
        low = jnp.min(jnp.where(rows_here, low, col_blocks))
        high = jnp.max(jnp.where(rows_here, high, 0))
        return jnp.where(low < col_blocks, low, 0), high

    for j in range(nb):
        for u, block in enumerate(extremes(c ^ j, c)):
            picks_ref[j, :, u * blk:(u + 1) * blk] = c_ref[:, pl.ds(pl.multiple_of(block * blk, blk), blk)]
    for owner in range(nb):
        small[2 * na + owner] = extremes(c, owner)[0]
    for n in range(2 * na):
        small[n] = 0
    for side in range(2):
        receiver = a ^ side
        for k in range(ops):
            for i in range(row_blocks):
                for s in range(slots):
                    entry = a_lists[s, k, receiver * row_blocks + i]
                    owner = lax.div(entry, row_blocks)
                    small[side * na + owner] = entry - owner * row_blocks


def sigma_kernel(geometry, small, a_lists, a_counts, b_lists, b_counts, picks, a_hbm, b_hbm, out_ref, abuf, bbuf, column, across, chosen, adense, bdense, acc,
                 local_sem, beta_send, beta_recv, column_recv, up_send, down_send, across_send, across_recv):
    na, nb, ops, slots, blk, row_blocks, col_blocks = geometry
    levels = na // PAIR
    rows = row_blocks * blk
    wide = FROM_B * blk
    a = lax.axis_index("alpha")
    c = lax.axis_index("beta")
    z = a // PAIR
    x = a % PAIR
    partner = a + 1 - 2 * x
    at_low = 2 * na

    def one_hot(value, place):
        gap = value - place
        return (1 - jnp.minimum(jnp.maximum(gap, -gap), 1)).astype(jnp.float32)

    def at_most(slot, count):
        return jnp.minimum(jnp.maximum(count - slot, 0), 1)

    copy_a = pltpu.make_async_copy(a_hbm, abuf, local_sem.at[0])
    copy_b = pltpu.make_async_copy(b_hbm, bbuf, local_sem.at[1])
    copy_a.start()
    copy_b.start()

    column[z, 0] = picks[0]

    barrier = pltpu.get_barrier_semaphore()
    for j in range(1, nb):
        pl.semaphore_signal(barrier, inc=1, device_id={"beta": c ^ j}, device_id_type=MESH)
    pl.semaphore_signal(barrier, inc=1, device_id={"alpha": partner}, device_id_type=MESH)

    @pl.when(z < levels - 1)
    def _():
        pl.semaphore_signal(barrier, inc=1, device_id={"alpha": a + PAIR}, device_id_type=MESH)

    @pl.when(z > 0)
    def _():
        pl.semaphore_signal(barrier, inc=1, device_id={"alpha": a - PAIR}, device_id_type=MESH)

    neighbours = nb + jnp.where(z < levels - 1, 1, 0) + jnp.where(z > 0, 1, 0)
    pl.semaphore_wait(barrier, neighbours)

    def beta_copy(j):
        return pltpu.make_async_remote_copy(
            src_ref=picks.at[j], dst_ref=column.at[z, j], send_sem=beta_send.at[j - 1], recv_sem=beta_recv.at[j - 1],
            device_id={"beta": c ^ j}, device_id_type=MESH)

    def up_copy(lev, j):
        return pltpu.make_async_remote_copy(
            src_ref=column.at[lev, j], dst_ref=column.at[lev, j], send_sem=up_send.at[lev, j], recv_sem=column_recv.at[lev, j],
            device_id={"alpha": a + PAIR}, device_id_type=MESH)

    def down_copy(lev, j):
        return pltpu.make_async_remote_copy(
            src_ref=column.at[lev, j], dst_ref=column.at[lev, j], send_sem=down_send.at[lev, j], recv_sem=column_recv.at[lev, j],
            device_id={"alpha": a - PAIR}, device_id_type=MESH)

    def across_copy(lev, j):
        return pltpu.make_async_remote_copy(
            src_ref=chosen.at[lev, j], dst_ref=across.at[lev, j], send_sem=across_send.at[lev, j], recv_sem=across_recv.at[lev, j],
            device_id={"alpha": partner}, device_id_type=MESH)

    for j in range(1, nb):
        beta_copy(j).start()

    acc[...] = jnp.zeros_like(acc)
    out_ref[...] = jnp.zeros_like(out_ref)

    def build_a():
        copy_a.wait()

        def per_owner(o, carry):
            for k in range(ops):
                for i in range(row_blocks):
                    total = jnp.zeros((blk, blk), jnp.float32)
                    for s in range(slots):
                        entry = a_lists[s, k, a * row_blocks + i]
                        valid = at_most(s, a_counts[k, a * row_blocks + i])
                        weight = one_hot(lax.div(entry, row_blocks), o) * valid.astype(jnp.float32)
                        total += abuf[k, s, i * blk:(i + 1) * blk, :].astype(jnp.float32) * weight
                    high = total.astype(jnp.bfloat16)
                    low = (total - high.astype(jnp.float32)).astype(jnp.bfloat16)
                    at = k * rows + i * blk
                    adense[o, 0, at:at + blk, :] = high
                    adense[o, 1, at:at + blk, :] = low
            return carry

        lax.fori_loop(0, na, per_owner, 0)

    def build_b(piece):
        k = piece // col_blocks
        r = piece % col_blocks
        here = pl.ds(pl.multiple_of(r * blk, blk), blk)
        codes = []
        for s in range(slots):
            entry = b_lists[s, k, c * col_blocks + r]
            owner = lax.div(entry, col_blocks)
            gap = entry - owner * col_blocks - small[at_low + owner]
            place = (owner ^ c) * FROM_B + jnp.minimum(jnp.maximum(gap, -gap), 1)
            valid = at_most(s, b_counts[k, c * col_blocks + r])
            codes.append((place + 1) * valid - 1)

        def per_chunk(j, carry):
            for u in range(FROM_B):
                total = jnp.zeros((blk, blk), jnp.float32)
                for s in range(slots):
                    weight = one_hot(codes[s], j * FROM_B + u)
                    total += bbuf[k, s, here, :].astype(jnp.float32) * weight
                high = total.astype(jnp.bfloat16)
                low = (total - high.astype(jnp.float32)).astype(jnp.bfloat16)
                bdense[j, 0, k, here, u * blk:(u + 1) * blk] = high
                bdense[j, 1, k, here, u * blk:(u + 1) * blk] = low
            return carry

        lax.fori_loop(0, nb, per_chunk, 0)

    pieces = ops * col_blocks

    def selected(lev, j, pick):
        total = jnp.zeros((blk, wide), jnp.float32)
        for i in range(row_blocks):
            total += column[lev, j, i * blk:(i + 1) * blk, :].astype(jnp.float32) * one_hot(pick, i)
        return total.astype(jnp.bfloat16)

    wave = 2 * levels
    waves = levels + nb - 1

    def place_of(n):
        distance = (n // 2) % levels
        upper = n % 2
        j = n // wave - distance
        lev = z + distance * (2 * upper - 1)
        valid = (j >= 0) & (j < nb) & (lev >= 0) & (lev < levels) & (distance + 1 > upper)
        return lev, j, distance, valid

    def accumulate(owner, j, value):
        acc[j] += (jnp.dot(adense[owner, 0], value, preferred_element_type=jnp.float32)
                   + jnp.dot(adense[owner, 1], value, preferred_element_type=jnp.float32))

    def along(m):
        lev, j, distance, valid = place_of(m)

        @pl.when(valid)
        def _():
            @pl.when((distance == 0) & (j > 0))
            def _():
                pltpu.make_async_remote_copy(
                    src_ref=picks.at[1], dst_ref=column.at[z, j], send_sem=beta_send.at[0], recv_sem=beta_recv.at[jnp.maximum(j, 1) - 1],
                    device_id={"beta": c ^ 1}, device_id_type=MESH).wait_recv()

            @pl.when(distance > 0)
            def _():
                across_like = pltpu.make_async_remote_copy(
                    src_ref=column.at[lev, j], dst_ref=column.at[lev, j], send_sem=up_send.at[lev, j], recv_sem=column_recv.at[lev, j],
                    device_id={"alpha": partner}, device_id_type=MESH)
                across_like.wait_recv()

            @pl.when((lev <= z) & (z < levels - 1))
            def _():
                up_copy(lev, j).start()

            @pl.when((lev >= z) & (z > 0))
            def _():
                down_copy(lev, j).start()

            owner = lev * PAIR + x
            chosen[lev, j] = selected(lev, j, small[na + owner])

            @pl.when(m == 0)
            def _():
                build_a()

            accumulate(owner, j, selected(lev, j, small[owner]))
            across_copy(lev, j).start()

    def over(m):
        lev, j, distance, valid = place_of(m)

        @pl.when(valid)
        def _():
            across_copy(lev, j).wait_recv()
            accumulate(lev * PAIR + 1 - x, j, across[lev, j])

    steps = waves * wave
    tile = min(2, col_blocks) * blk

    def finish(j):
        inters = [acc[j, k * rows:(k + 1) * rows, :].astype(jnp.bfloat16) for k in range(ops)]

        def columns(n, carry):
            here = pl.ds(pl.multiple_of(n * tile, tile), tile)
            total = out_ref[:, here]
            for k in range(ops):
                for half in range(2):
                    total += lax.dot_general(inters[k], bdense[j, half, k, here, :], (((1,), (1,)), ((), ())),
                                             preferred_element_type=jnp.float32)
            out_ref[:, here] = total
            return carry

        lax.fori_loop(0, col_blocks * blk // tile, columns, 0)

    def step(m, carry):
        @pl.when(m < steps)
        def _():
            along(m)

        piece = m - wave

        @pl.when(piece == 0)
        def _():
            copy_b.wait()

        @pl.when((piece >= 0) & (piece < pieces))
        def _():
            build_b(piece)

        @pl.when(m >= wave)
        def _():
            over(m - wave)

        done = m // wave - levels

        @pl.when((m % wave == wave - 1) & (done >= 0))
        def _():
            finish(done)

        return carry

    lax.fori_loop(0, steps + wave, step, 0)

    for j in range(1, nb):
        beta_copy(j).wait_send()

    def drain(n, carry):
        lev = n // nb
        j = n % nb

        @pl.when((lev <= z) & (z < levels - 1))
        def _():
            up_copy(lev, j).wait_send()

        @pl.when((lev >= z) & (z > 0))
        def _():
            down_copy(lev, j).wait_send()

        across_copy(lev, j).wait_send()
        return carry

    lax.fori_loop(0, levels * nb, drain, 0)


def scratch_of(geometry, dtype):
    na, nb, ops, slots, blk, row_blocks, col_blocks = geometry
    levels = na // PAIR
    rows, cols, wide = row_blocks * blk, col_blocks * blk, FROM_B * blk
    return [
        ((ops, slots, rows, blk), dtype),
        ((ops, slots, cols, blk), dtype),
        ((levels, nb, rows, wide), dtype),
        ((levels, nb, blk, wide), dtype),
        ((levels, nb, blk, wide), dtype),
        ((na, 2, ops * rows, blk), dtype),
        ((nb, 2, ops, cols, wide), dtype),
        ((nb, ops * rows, wide), jnp.float32),
    ]


def scratch_bytes(geometry):
    total = 0
    for shape, dtype in scratch_of(geometry, jnp.bfloat16):
        size = jnp.dtype(dtype).itemsize
        for extent in shape:
            size *= extent
        total += size
    return total


def fused(geometry, coeffs, a_blocks, a_list, a_count, b_blocks, b_list, b_count):
    na, nb, ops, slots, blk, row_blocks, col_blocks = geometry
    levels = na // PAIR
    a_lists = jnp.transpose(a_list, (2, 0, 1))
    b_lists = jnp.transpose(b_list, (2, 0, 1))
    rows, cols = row_blocks * blk, col_blocks * blk
    dma = pltpu.SemaphoreType.DMA
    smem = pl.BlockSpec(memory_space=pltpu.SMEM)
    vmem = pl.BlockSpec(memory_space=pltpu.VMEM)
    picks, small = pl.pallas_call(
        functools.partial(pick_kernel, geometry),
        out_shape=(jax.ShapeDtypeStruct((nb, rows, FROM_B * blk), coeffs.dtype), jax.ShapeDtypeStruct((2 * na + nb,), jnp.int32)),
        in_specs=[smem, vmem, vmem],
        out_specs=(vmem, smem),
        name="pick_blocks",
    )(a_lists, b_lists, coeffs)
    return pl.pallas_call(
        functools.partial(sigma_kernel, geometry),
        out_shape=jax.ShapeDtypeStruct((rows, cols), jnp.float32),
        in_specs=[
            smem, smem, smem, smem, smem, vmem,
            pl.BlockSpec(memory_space=pl.ANY),
            pl.BlockSpec(memory_space=pl.ANY),
        ],
        out_specs=pl.BlockSpec(memory_space=pltpu.VMEM),
        scratch_shapes=[pltpu.VMEM(shape, dtype) for shape, dtype in scratch_of(geometry, coeffs.dtype)] + [
            dma((2,)), dma((nb - 1,)), dma((nb - 1,)), dma((levels, nb)), dma((levels, nb)), dma((levels, nb)),
            dma((levels, nb)), dma((levels, nb)),
        ],
        compiler_params=pltpu.CompilerParams(collective_id=0, has_side_effects=True, vmem_limit_bytes=VMEM_LIMIT),
        name="sigma_build",
    )(small, a_lists, a_count, b_lists, b_count, picks, jnp.transpose(a_blocks, (0, 2, 1, 3)), jnp.transpose(b_blocks, (0, 2, 1, 3)))


def arrange(entries, owners, per_owner, capacity):
    operators, total, list_slots = entries.shape
    flattened = entries.reshape(operators, owners, per_owner * list_slots)
    matches = flattened[..., None] == jnp.arange(total, dtype=jnp.int32)
    present = jnp.any(matches, axis=(0, 2)).reshape(owners, owners, per_owner).astype(jnp.int32)
    ranking = jnp.cumsum(present, axis=2)
    position = jnp.arange(capacity, dtype=jnp.int32) + 1
    chosen_bits = (present[..., None] == 1) & (ranking[..., None] == position)
    local_ids = jnp.arange(per_owner, dtype=jnp.int32)[None, None, :, None]
    wanted = jnp.sum(local_ids * chosen_bits.astype(jnp.int32), axis=2)
    return (wanted, ranking)


def locate(entries, ranking_here, per_owner, capacity):
    owner = entries // per_owner
    local_id = entries % per_owner
    return owner * capacity + ranking_here[owner, local_id] - 1


def pick_columns(pool_piece, index_piece):
    return pool_piece[:, index_piece]


def plain(coeffs, a_blocks, a_list, a_count, b_blocks, b_list, b_count):
    operators, local_rows, list_slots, block_size = a_blocks.shape
    local_cols = coeffs.shape[1]
    row_blocks = local_rows // block_size
    col_blocks = local_cols // block_size
    row_capacity = FROM_A
    col_capacity = FROM_B
    alpha_size = lax.axis_size("alpha")
    beta_size = lax.axis_size("beta")
    alpha_here = lax.axis_index("alpha")
    beta_here = lax.axis_index("beta")
    slot_ids = jnp.arange(list_slots, dtype=jnp.int32)
    alpha_mine = lax.dynamic_slice_in_dim(a_list, alpha_here * row_blocks, row_blocks, 1)
    alpha_counts = lax.dynamic_slice_in_dim(a_count, alpha_here * row_blocks, row_blocks, 1)
    alpha_valid = slot_ids < alpha_counts[..., None]
    alpha_kept = jnp.where(
        alpha_valid[:, :, None, :, None],
        a_blocks.reshape(operators, row_blocks, block_size, list_slots, block_size),
        jnp.zeros((), jnp.bfloat16),
    )
    wanted, ranking = arrange(a_list, alpha_size, row_blocks, row_capacity)
    outgoing = coeffs.reshape(row_blocks, block_size, local_cols)[wanted[:, alpha_here, :]]
    incoming = lax.all_to_all(outgoing, "alpha", split_axis=0, concat_axis=0, tiled=True)
    source_index = locate(alpha_mine, ranking[alpha_here], row_blocks, row_capacity)
    chosen = incoming.reshape(alpha_size * row_capacity, block_size, local_cols)[source_index]
    inter = jnp.einsum("kbrsi,kbsic->kbrc", alpha_kept, chosen, preferred_element_type=jnp.float32)
    inter = inter.astype(jnp.bfloat16).reshape(operators, local_rows, col_blocks, block_size)
    wanted_cols, ranking_cols = arrange(b_list, beta_size, col_blocks, col_capacity)
    outgoing_cols = inter[:, :, wanted_cols[:, beta_here, :], :]
    incoming_cols = lax.all_to_all(outgoing_cols, "beta", split_axis=2, concat_axis=2, tiled=True)
    beta_mine = lax.dynamic_slice_in_dim(b_list, beta_here * col_blocks, col_blocks, 1)
    beta_counts = lax.dynamic_slice_in_dim(b_count, beta_here * col_blocks, col_blocks, 1)
    beta_valid = slot_ids < beta_counts[..., None]
    beta_kept = jnp.where(
        beta_valid[:, :, None, :, None],
        b_blocks.reshape(operators, col_blocks, block_size, list_slots, block_size),
        jnp.zeros((), jnp.bfloat16),
    )
    source_cols = locate(beta_mine, ranking_cols[beta_here], col_blocks, col_capacity)
    pooled = incoming_cols.reshape(operators, local_rows, beta_size * col_capacity, block_size)
    picked = jax.vmap(pick_columns)(pooled, source_cols)
    sigma = jnp.einsum("kabsj,kbrsj->abr", picked, beta_kept, preferred_element_type=jnp.float32)
    return sigma.reshape(local_rows, local_cols)


def on_device(coeffs, a_blocks, a_list, a_count, b_blocks, b_list, b_count):
    operators, local_rows, list_slots, block_size = a_blocks.shape
    na, nb = lax.axis_size("alpha"), lax.axis_size("beta")
    geometry = (na, nb, operators, list_slots, block_size, local_rows // block_size, coeffs.shape[1] // block_size)
    fits = scratch_bytes(geometry) < VMEM_LIMIT * 3 // 4
    shaped = FROM_A == 1 and FROM_B == 2 and na % PAIR == 0 and nb & (nb - 1) == 0 and nb > 1
    build = functools.partial(fused, geometry) if fits and shaped else plain
    return build(coeffs, a_blocks, a_list, a_count, b_blocks, b_list, b_count)


def solution(mesh):
    in_specs = (
        P("alpha", "beta"),
        P(None, "alpha", None, None),
        P(),
        P(),
        P(None, "beta", None, None),
        P(),
        P(),
    )
    out_specs = P("alpha", "beta")
    return jax.shard_map(
        on_device, mesh=mesh, in_specs=in_specs, out_specs=out_specs, check_vma=False
    )
```

```python
import functools

import jax
import jax.numpy as jnp
from jax import lax
from jax.experimental import pallas as pl
from jax.experimental.pallas import tpu as pltpu
from jax.sharding import PartitionSpec as P

FROM_A = 1
FROM_B = 2
PAIR = 2
VMEM_LIMIT = 60 * 1024 * 1024
MESH = pl.DeviceIdType.MESH


def pick_kernel(geometry, a_lists, b_lists, c_ref, picks_ref, small):
    na, nb, ops, slots, blk, row_blocks, col_blocks = geometry
    a = lax.axis_index("alpha")
    c = lax.axis_index("beta")
    lists = b_lists[...]
    lane = lax.broadcasted_iota(jnp.int32, (1, nb * col_blocks), 1)

    def extremes(receiver, owner):
        local = lists - owner * col_blocks
        hit = (local >= 0) & (local < col_blocks)
        rows_here = (lane >= receiver * col_blocks) & (lane < (receiver + 1) * col_blocks)
        low = jnp.min(jnp.min(jnp.where(hit, local, col_blocks), axis=0), axis=0, keepdims=True)
        high = jnp.max(jnp.max(jnp.where(hit, local, 0), axis=0), axis=0, keepdims=True)
        low = jnp.min(jnp.where(rows_here, low, col_blocks))
        high = jnp.max(jnp.where(rows_here, high, 0))
        return jnp.where(low < col_blocks, low, 0), high

    for j in range(nb):
        for u, block in enumerate(extremes(c ^ j, c)):
            picks_ref[j, :, u * blk:(u + 1) * blk] = c_ref[:, pl.ds(pl.multiple_of(block * blk, blk), blk)]
    for owner in range(nb):
        small[2 * na + owner] = extremes(c, owner)[0]
    for n in range(2 * na):
        small[n] = 0
    for side in range(2):
        receiver = a ^ side
        for k in range(ops):
            for i in range(row_blocks):
                for s in range(slots):
                    entry = a_lists[s, k, receiver * row_blocks + i]
                    owner = lax.div(entry, row_blocks)
                    small[side * na + owner] = entry - owner * row_blocks


def sigma_kernel(geometry, small, a_lists, a_counts, b_lists, b_counts, picks, a_hbm, b_hbm, out_ref, abuf, bbuf, column, across, chosen, adense, bdense, acc,
                 local_sem, beta_send, beta_recv, column_recv, up_send, down_send, across_send, across_recv):
    na, nb, ops, slots, blk, row_blocks, col_blocks = geometry
    levels = na // PAIR
    rows = row_blocks * blk
    wide = FROM_B * blk
    a = lax.axis_index("alpha")
    c = lax.axis_index("beta")
    z = a // PAIR
    x = a % PAIR
    partner = a + 1 - 2 * x
    at_low = 2 * na

    def one_hot(value, place):
        gap = value - place
        return (1 - jnp.minimum(jnp.maximum(gap, -gap), 1)).astype(jnp.float32)

    def at_most(slot, count):
        return jnp.minimum(jnp.maximum(count - slot, 0), 1)

    copy_a = pltpu.make_async_copy(a_hbm, abuf, local_sem.at[0])
    copy_b = pltpu.make_async_copy(b_hbm, bbuf, local_sem.at[1])
    copy_a.start()
    copy_b.start()

    column[z, 0] = picks[0]

    barrier = pltpu.get_barrier_semaphore()
    for j in range(1, nb):
        pl.semaphore_signal(barrier, inc=1, device_id={"beta": c ^ j}, device_id_type=MESH)
    pl.semaphore_signal(barrier, inc=1, device_id={"alpha": partner}, device_id_type=MESH)

    @pl.when(z < levels - 1)
    def _():
        pl.semaphore_signal(barrier, inc=1, device_id={"alpha": a + PAIR}, device_id_type=MESH)

    @pl.when(z > 0)
    def _():
        pl.semaphore_signal(barrier, inc=1, device_id={"alpha": a - PAIR}, device_id_type=MESH)

    neighbours = nb + jnp.where(z < levels - 1, 1, 0) + jnp.where(z > 0, 1, 0)
    pl.semaphore_wait(barrier, neighbours)

    def beta_copy(j):
        return pltpu.make_async_remote_copy(
            src_ref=picks.at[j], dst_ref=column.at[z, j], send_sem=beta_send.at[j - 1], recv_sem=beta_recv.at[j - 1],
            device_id={"beta": c ^ j}, device_id_type=MESH)

    def up_copy(lev, j):
        return pltpu.make_async_remote_copy(
            src_ref=column.at[lev, j], dst_ref=column.at[lev, j], send_sem=up_send.at[lev, j], recv_sem=column_recv.at[lev, j],
            device_id={"alpha": a + PAIR}, device_id_type=MESH)

    def down_copy(lev, j):
        return pltpu.make_async_remote_copy(
            src_ref=column.at[lev, j], dst_ref=column.at[lev, j], send_sem=down_send.at[lev, j], recv_sem=column_recv.at[lev, j],
            device_id={"alpha": a - PAIR}, device_id_type=MESH)

    def across_copy(lev, j):
        return pltpu.make_async_remote_copy(
            src_ref=chosen.at[lev, j], dst_ref=across.at[lev, j], send_sem=across_send.at[lev, j], recv_sem=across_recv.at[lev, j],
            device_id={"alpha": partner}, device_id_type=MESH)

    for j in range(1, nb):
        beta_copy(j).start()

    acc[...] = jnp.zeros_like(acc)
    out_ref[...] = jnp.zeros_like(out_ref)

    def build_a():
        copy_a.wait()

        def per_owner(o, carry):
            for k in range(ops):
                for i in range(row_blocks):
                    total = jnp.zeros((blk, blk), jnp.float32)
                    for s in range(slots):
                        entry = a_lists[s, k, a * row_blocks + i]
                        valid = at_most(s, a_counts[k, a * row_blocks + i])
                        weight = one_hot(lax.div(entry, row_blocks), o) * valid.astype(jnp.float32)
                        total += abuf[k, s, i * blk:(i + 1) * blk, :].astype(jnp.float32) * weight
                    high = total.astype(jnp.bfloat16)
                    low = (total - high.astype(jnp.float32)).astype(jnp.bfloat16)
                    at = k * rows + i * blk
                    adense[o, 0, at:at + blk, :] = high
                    adense[o, 1, at:at + blk, :] = low
            return carry

        lax.fori_loop(0, na, per_owner, 0)

    def build_b(piece):
        k = piece // col_blocks
        r = piece % col_blocks
        here = pl.ds(pl.multiple_of(r * blk, blk), blk)
        codes = []
        for s in range(slots):
            entry = b_lists[s, k, c * col_blocks + r]
            owner = lax.div(entry, col_blocks)
            gap = entry - owner * col_blocks - small[at_low + owner]
            place = (owner ^ c) * FROM_B + jnp.minimum(jnp.maximum(gap, -gap), 1)
            valid = at_most(s, b_counts[k, c * col_blocks + r])
            codes.append((place + 1) * valid - 1)

        def per_chunk(j, carry):
            for u in range(FROM_B):
                total = jnp.zeros((blk, blk), jnp.float32)
                for s in range(slots):
                    weight = one_hot(codes[s], j * FROM_B + u)
                    total += bbuf[k, s, here, :].astype(jnp.float32) * weight
                high = total.astype(jnp.bfloat16)
                low = (total - high.astype(jnp.float32)).astype(jnp.bfloat16)
                bdense[j, 0, k, here, u * blk:(u + 1) * blk] = high
                bdense[j, 1, k, here, u * blk:(u + 1) * blk] = low
            return carry

        lax.fori_loop(0, nb, per_chunk, 0)

    pieces = ops * col_blocks

    def selected(lev, j, pick):
        total = jnp.zeros((blk, wide), jnp.float32)
        for i in range(row_blocks):
            total += column[lev, j, i * blk:(i + 1) * blk, :].astype(jnp.float32) * one_hot(pick, i)
        return total.astype(jnp.bfloat16)

    wave = 2 * levels
    waves = levels + nb - 1

    def place_of(n):
        distance = (n // 2) % levels
        upper = n % 2
        j = n // wave - distance
        lev = z + distance * (2 * upper - 1)
        valid = (j >= 0) & (j < nb) & (lev >= 0) & (lev < levels) & (distance + 1 > upper)
        return lev, j, distance, valid

    def accumulate(owner, j, value):
        acc[j] += (jnp.dot(adense[owner, 0], value, preferred_element_type=jnp.float32)
                   + jnp.dot(adense[owner, 1], value, preferred_element_type=jnp.float32))

    def along(m):
        lev, j, distance, valid = place_of(m)

        @pl.when(valid)
        def _():
            @pl.when((distance == 0) & (j > 0))
            def _():
                pltpu.make_async_remote_copy(
                    src_ref=picks.at[1], dst_ref=column.at[z, j], send_sem=beta_send.at[0], recv_sem=beta_recv.at[jnp.maximum(j, 1) - 1],
                    device_id={"beta": c ^ 1}, device_id_type=MESH).wait_recv()

            @pl.when(distance > 0)
            def _():
                across_like = pltpu.make_async_remote_copy(
                    src_ref=column.at[lev, j], dst_ref=column.at[lev, j], send_sem=up_send.at[lev, j], recv_sem=column_recv.at[lev, j],
                    device_id={"alpha": partner}, device_id_type=MESH)
                across_like.wait_recv()

            owner = lev * PAIR + x
            chosen[lev, j] = selected(lev, j, small[na + owner])

            @pl.when((lev <= z) & (z < levels - 1))
            def _():
                up_copy(lev, j).start()

            @pl.when((lev >= z) & (z > 0))
            def _():
                down_copy(lev, j).start()

            across_copy(lev, j).start()

            @pl.when(m == 0)
            def _():
                build_a()

            accumulate(owner, j, selected(lev, j, small[owner]))

    def over(m):
        lev, j, distance, valid = place_of(m)

        @pl.when(valid)
        def _():
            across_copy(lev, j).wait_recv()
            accumulate(lev * PAIR + 1 - x, j, across[lev, j])

    steps = waves * wave
    tile = min(2, col_blocks) * blk

    def finish(j):
        inters = [acc[j, k * rows:(k + 1) * rows, :].astype(jnp.bfloat16) for k in range(ops)]

        def columns(n, carry):
            here = pl.ds(pl.multiple_of(n * tile, tile), tile)
            total = out_ref[:, here]
            for k in range(ops):
                for half in range(2):
                    total += lax.dot_general(inters[k], bdense[j, half, k, here, :], (((1,), (1,)), ((), ())),
                                             preferred_element_type=jnp.float32)
            out_ref[:, here] = total
            return carry

        lax.fori_loop(0, col_blocks * blk // tile, columns, 0)

    def step(m, carry):
        @pl.when(m < steps)
        def _():
            along(m)

        piece = m - wave

        @pl.when(piece == 0)
        def _():
            copy_b.wait()

        @pl.when((piece >= 0) & (piece < pieces))
        def _():
            build_b(piece)

        @pl.when(m >= wave)
        def _():
            over(m - wave)

        done = m // wave - levels

        @pl.when((m % wave == wave - 1) & (done >= 0))
        def _():
            finish(done)

        return carry

    lax.fori_loop(0, steps + wave, step, 0)

    for j in range(1, nb):
        beta_copy(j).wait_send()

    def drain(n, carry):
        lev = n // nb
        j = n % nb

        @pl.when((lev <= z) & (z < levels - 1))
        def _():
            up_copy(lev, j).wait_send()

        @pl.when((lev >= z) & (z > 0))
        def _():
            down_copy(lev, j).wait_send()

        across_copy(lev, j).wait_send()
        return carry

    lax.fori_loop(0, levels * nb, drain, 0)


def scratch_of(geometry, dtype):
    na, nb, ops, slots, blk, row_blocks, col_blocks = geometry
    levels = na // PAIR
    rows, cols, wide = row_blocks * blk, col_blocks * blk, FROM_B * blk
    return [
        ((ops, slots, rows, blk), dtype),
        ((ops, slots, cols, blk), dtype),
        ((levels, nb, rows, wide), dtype),
        ((levels, nb, blk, wide), dtype),
        ((levels, nb, blk, wide), dtype),
        ((na, 2, ops * rows, blk), dtype),
        ((nb, 2, ops, cols, wide), dtype),
        ((nb, ops * rows, wide), jnp.float32),
    ]


def scratch_bytes(geometry):
    total = 0
    for shape, dtype in scratch_of(geometry, jnp.bfloat16):
        size = jnp.dtype(dtype).itemsize
        for extent in shape:
            size *= extent
        total += size
    return total


def fused(geometry, coeffs, a_blocks, a_list, a_count, b_blocks, b_list, b_count):
    na, nb, ops, slots, blk, row_blocks, col_blocks = geometry
    levels = na // PAIR
    a_lists = jnp.transpose(a_list, (2, 0, 1))
    b_lists = jnp.transpose(b_list, (2, 0, 1))
    rows, cols = row_blocks * blk, col_blocks * blk
    dma = pltpu.SemaphoreType.DMA
    smem = pl.BlockSpec(memory_space=pltpu.SMEM)
    vmem = pl.BlockSpec(memory_space=pltpu.VMEM)
    picks, small = pl.pallas_call(
        functools.partial(pick_kernel, geometry),
        out_shape=(jax.ShapeDtypeStruct((nb, rows, FROM_B * blk), coeffs.dtype), jax.ShapeDtypeStruct((2 * na + nb,), jnp.int32)),
        in_specs=[smem, vmem, vmem],
        out_specs=(vmem, smem),
        name="pick_blocks",
    )(a_lists, b_lists, coeffs)
    return pl.pallas_call(
        functools.partial(sigma_kernel, geometry),
        out_shape=jax.ShapeDtypeStruct((rows, cols), jnp.float32),
        in_specs=[
            smem, smem, smem, smem, smem, vmem,
            pl.BlockSpec(memory_space=pl.ANY),
            pl.BlockSpec(memory_space=pl.ANY),
        ],
        out_specs=pl.BlockSpec(memory_space=pltpu.VMEM),
        scratch_shapes=[pltpu.VMEM(shape, dtype) for shape, dtype in scratch_of(geometry, coeffs.dtype)] + [
            dma((2,)), dma((nb - 1,)), dma((nb - 1,)), dma((levels, nb)), dma((levels, nb)), dma((levels, nb)),
            dma((levels, nb)), dma((levels, nb)),
        ],
        compiler_params=pltpu.CompilerParams(collective_id=0, has_side_effects=True, vmem_limit_bytes=VMEM_LIMIT),
        name="sigma_build",
    )(small, a_lists, a_count, b_lists, b_count, picks, jnp.transpose(a_blocks, (0, 2, 1, 3)), jnp.transpose(b_blocks, (0, 2, 1, 3)))


def arrange(entries, owners, per_owner, capacity):
    operators, total, list_slots = entries.shape
    flattened = entries.reshape(operators, owners, per_owner * list_slots)
    matches = flattened[..., None] == jnp.arange(total, dtype=jnp.int32)
    present = jnp.any(matches, axis=(0, 2)).reshape(owners, owners, per_owner).astype(jnp.int32)
    ranking = jnp.cumsum(present, axis=2)
    position = jnp.arange(capacity, dtype=jnp.int32) + 1
    chosen_bits = (present[..., None] == 1) & (ranking[..., None] == position)
    local_ids = jnp.arange(per_owner, dtype=jnp.int32)[None, None, :, None]
    wanted = jnp.sum(local_ids * chosen_bits.astype(jnp.int32), axis=2)
    return (wanted, ranking)


def locate(entries, ranking_here, per_owner, capacity):
    owner = entries // per_owner
    local_id = entries % per_owner
    return owner * capacity + ranking_here[owner, local_id] - 1


def pick_columns(pool_piece, index_piece):
    return pool_piece[:, index_piece]


def plain(coeffs, a_blocks, a_list, a_count, b_blocks, b_list, b_count):
    operators, local_rows, list_slots, block_size = a_blocks.shape
    local_cols = coeffs.shape[1]
    row_blocks = local_rows // block_size
    col_blocks = local_cols // block_size
    row_capacity = FROM_A
    col_capacity = FROM_B
    alpha_size = lax.axis_size("alpha")
    beta_size = lax.axis_size("beta")
    alpha_here = lax.axis_index("alpha")
    beta_here = lax.axis_index("beta")
    slot_ids = jnp.arange(list_slots, dtype=jnp.int32)
    alpha_mine = lax.dynamic_slice_in_dim(a_list, alpha_here * row_blocks, row_blocks, 1)
    alpha_counts = lax.dynamic_slice_in_dim(a_count, alpha_here * row_blocks, row_blocks, 1)
    alpha_valid = slot_ids < alpha_counts[..., None]
    alpha_kept = jnp.where(
        alpha_valid[:, :, None, :, None],
        a_blocks.reshape(operators, row_blocks, block_size, list_slots, block_size),
        jnp.zeros((), jnp.bfloat16),
    )
    wanted, ranking = arrange(a_list, alpha_size, row_blocks, row_capacity)
    outgoing = coeffs.reshape(row_blocks, block_size, local_cols)[wanted[:, alpha_here, :]]
    incoming = lax.all_to_all(outgoing, "alpha", split_axis=0, concat_axis=0, tiled=True)
    source_index = locate(alpha_mine, ranking[alpha_here], row_blocks, row_capacity)
    chosen = incoming.reshape(alpha_size * row_capacity, block_size, local_cols)[source_index]
    inter = jnp.einsum("kbrsi,kbsic->kbrc", alpha_kept, chosen, preferred_element_type=jnp.float32)
    inter = inter.astype(jnp.bfloat16).reshape(operators, local_rows, col_blocks, block_size)
    wanted_cols, ranking_cols = arrange(b_list, beta_size, col_blocks, col_capacity)
    outgoing_cols = inter[:, :, wanted_cols[:, beta_here, :], :]
    incoming_cols = lax.all_to_all(outgoing_cols, "beta", split_axis=2, concat_axis=2, tiled=True)
    beta_mine = lax.dynamic_slice_in_dim(b_list, beta_here * col_blocks, col_blocks, 1)
    beta_counts = lax.dynamic_slice_in_dim(b_count, beta_here * col_blocks, col_blocks, 1)
    beta_valid = slot_ids < beta_counts[..., None]
    beta_kept = jnp.where(
        beta_valid[:, :, None, :, None],
        b_blocks.reshape(operators, col_blocks, block_size, list_slots, block_size),
        jnp.zeros((), jnp.bfloat16),
    )
    source_cols = locate(beta_mine, ranking_cols[beta_here], col_blocks, col_capacity)
    pooled = incoming_cols.reshape(operators, local_rows, beta_size * col_capacity, block_size)
    picked = jax.vmap(pick_columns)(pooled, source_cols)
    sigma = jnp.einsum("kabsj,kbrsj->abr", picked, beta_kept, preferred_element_type=jnp.float32)
    return sigma.reshape(local_rows, local_cols)


def on_device(coeffs, a_blocks, a_list, a_count, b_blocks, b_list, b_count):
    operators, local_rows, list_slots, block_size = a_blocks.shape
    na, nb = lax.axis_size("alpha"), lax.axis_size("beta")
    geometry = (na, nb, operators, list_slots, block_size, local_rows // block_size, coeffs.shape[1] // block_size)
    fits = scratch_bytes(geometry) < VMEM_LIMIT * 3 // 4
    shaped = FROM_A == 1 and FROM_B == 2 and na % PAIR == 0 and nb & (nb - 1) == 0 and nb > 1
    build = functools.partial(fused, geometry) if fits and shaped else plain
    return build(coeffs, a_blocks, a_list, a_count, b_blocks, b_list, b_count)


def solution(mesh):
    in_specs = (
        P("alpha", "beta"),
        P(None, "alpha", None, None),
        P(),
        P(),
        P(None, "beta", None, None),
        P(),
        P(),
    )
    out_specs = P("alpha", "beta")
    return jax.shard_map(
        on_device, mesh=mesh, in_specs=in_specs, out_specs=out_specs, check_vma=False
    )
```
